32 devices in a mesh: groups: 2 (over y), seq: 8 (over z, x), enc: 2 (over core).
Axes of the slice: x: 2, y: 2, z: 4, core: 2. Of those that a mesh axis runs over, the one named last changes fastest.
Arguments:
- self_queries: bfloat16 [2, 256, 4096], P('enc', ('groups', 'seq')), parts along dimension 1, may hold values from -32 to 32
- self_keys: bfloat16 [2, 256, 4096], P('enc', ('groups', 'seq')), parts along dimension 1, may hold values from -32 to 32
- self_values: bfloat16 [2, 256, 4096], P('enc', ('groups', 'seq')), parts along dimension 1, may hold values from -6 to 6
- text_queries: bfloat16 [2, 256, 4096], P('enc', ('groups', 'seq')), parts along dimension 1, may hold values from -32 to 32
- text_kv: bfloat16 [2, 2, 1024, 4096], P('enc', None, ('groups', 'seq')), parts along dimension 2, may hold values from -32 to 32
- text_len: int32 [4], P('groups'), parts along dimension 0, may hold values from 16 to 512
Outputs:
- self_mixed: bfloat16 [2, 256, 4096], P('enc', ('groups', 'seq')), parts along dimension 1
- text_mixed: bfloat16 [2, 256, 4096], P('enc', ('groups', 'seq')), parts along dimension 1
The draws below stay inside these ranges and needn't reach their ends.
There are 2 independent parts, one for each index of `groups`. The reference program is written for one: setup_inputs(seed, part) draws one part's arguments, and reference() takes and returns one part's arrays. A program takes and returns all parts, laid end to end along the dimension named above; each array names one. Nothing has to cross between parts.
Inputs may be any that keep to these rules, and one draw needn't show every extreme that they name: `text_len`: entry 0 is the prompt's length, entry 1 the negative prompt's; text rows at or past a length are padding.
All inputs are finite; a program needn't handle non-finite values.
Results may differ from the reference program's by a relative error of at most 0.0034.
Values may be sent and summed in bfloat16 or wider, within the bound.
A program may use at most 64 MiB of HBM per device.

```python
import math
import jax
import jax.numpy as jnp
from jax import lax

HEADS = 32
HEAD_DIM = 128
TEXT = 512
SEQ = 128
CHANNELS = 4096


def row_scaled(key, shape, scale):
    base = scale * jax.random.truncated_normal(jax.random.fold_in(key, 1), -4.0, 4.0, shape, jnp.float32)
    return base


def draw_self_queries(key, part):
    queries = row_scaled(jax.random.fold_in(key, 11), (2, SEQ, CHANNELS), 1.6)
    return queries.astype(jnp.bfloat16)


def draw_self_keys(key, part):
    key_table = row_scaled(jax.random.fold_in(key, 12), (2, SEQ, CHANNELS), 1.6)
    return key_table.astype(jnp.bfloat16)


def draw_text_queries(key, part):
    queries = row_scaled(jax.random.fold_in(key, 13), (2, SEQ, CHANNELS), 1.6)
    return queries.astype(jnp.bfloat16)


def draw_text_kv(key, part):
    key_table = row_scaled(jax.random.fold_in(key, 14), (2, TEXT, CHANNELS), 1.6)
    value_table = jax.random.truncated_normal(jax.random.fold_in(key, 15), -4.0, 4.0, (2, TEXT, CHANNELS), jnp.float32)
    return jnp.stack([key_table, value_table], axis=1).astype(jnp.bfloat16)


def block_levels(stream_key, dims, cuts, low, largest):
    loudness, own = 1.0, jax.random.fold_in(stream_key, 6)
    for position, blocks in cuts:
        steps = jnp.exp(jax.random.uniform(jax.random.fold_in(own, position), (blocks,), jnp.float32, low / len(cuts), largest / len(cuts)))
        loudness = loudness * jnp.repeat(steps, dims[position] // blocks).reshape([-1 if axis == position else 1 for axis in range(len(dims))])
    return loudness


def gaussian(stream_key, dims, scale, limit, shards=(), held_as=jnp.bfloat16):
    entries = scale * jax.random.normal(stream_key, dims, jnp.float32)
    if shards:
        entries = entries * block_levels(stream_key, dims, shards, -0.22, 0.18)
    return jnp.clip(entries, -limit, limit).astype(held_as)


def setup_inputs(seed: int = 0, part: int = 0) -> dict:
    key_list = jax.random.split(jax.random.key(seed), 7)
    own_keys = jax.random.split(jax.random.fold_in(key_list[6], part), 7)
    self_queries = draw_self_queries(jax.random.fold_in(jax.random.fold_in(key_list[6], part), 71), part)
    self_keys = draw_self_keys(jax.random.fold_in(jax.random.fold_in(key_list[6], part), 71), part)
    self_values = gaussian(own_keys[2], (2, SEQ, CHANNELS), 1.0, 6.0, ((0, 2), (1, 8)))
    text_queries = draw_text_queries(jax.random.fold_in(jax.random.fold_in(key_list[6], part), 71), part)
    text_kv = draw_text_kv(jax.random.fold_in(jax.random.fold_in(key_list[6], part), 71), part)
    text_len = jax.random.randint(own_keys[5], (2,), 16, TEXT + 1).astype(jnp.int32)
    return dict(self_queries=self_queries, self_keys=self_keys, self_values=self_values, text_queries=text_queries, text_kv=text_kv, text_len=text_len)


def head_attention(query_rows, key_rows, value_rows, live_mask):
    scores = jnp.dot(query_rows, key_rows.T, preferred_element_type=jnp.float32) / math.sqrt(HEAD_DIM)
    scores = jnp.where(live_mask[None, :], scores, -1e+30)
    shifted = jnp.where(live_mask[None, :], jnp.exp(scores - lax.optimization_barrier(jnp.max(scores, axis=1, keepdims=True))), 0.0)
    blended = jnp.dot(shifted.astype(jnp.bfloat16), value_rows, preferred_element_type=jnp.float32)
    return (blended / lax.optimization_barrier(jnp.sum(shifted, axis=1, keepdims=True))).astype(jnp.bfloat16)

def by_heads(tensor):
    return tensor.reshape(tensor.shape[0], HEADS, HEAD_DIM).transpose(1, 0, 2)

def from_heads(tensor):
    return tensor.transpose(1, 0, 2).reshape(tensor.shape[1], HEADS * HEAD_DIM)

def attend_all(queries, key_rows, value_rows, live_mask):

    def one_head(triple):
        return head_attention(triple[0], triple[1], triple[2], live_mask)
    return from_heads(lax.map(one_head, (by_heads(queries), by_heads(key_rows), by_heads(value_rows))))

def reference(self_queries, self_keys, self_values, text_queries, text_kv, text_len):
    self_list = []
    text_list = []
    positions = jnp.arange(TEXT, dtype=jnp.int32)
    every_key = jnp.ones((SEQ,), jnp.bool_)
    for branch in range(2):
        self_list.append(attend_all(self_queries[branch], self_keys[branch], self_values[branch], every_key))
        live_mask = positions < text_len[branch]
        text_list.append(attend_all(text_queries[branch], text_kv[branch, 0], text_kv[branch, 1], live_mask))
    return (jnp.stack(self_list), jnp.stack(text_list))
```

```python
import functools
import math

import jax
import jax.numpy as jnp
from jax import lax
from jax.experimental import pallas as pl
from jax.experimental.pallas import tpu as pltpu
from jax.sharding import PartitionSpec as P

HEADS = 32
HEAD_DIM = 128


def absorb(run_state, queries, key_rows, value_rows, live_mask):
    running_max, row_total, weighted_sum = run_state
    scores = jnp.einsum(
        "qpd,kpd->pqk", queries, key_rows, preferred_element_type=jnp.float32
    ) / math.sqrt(HEAD_DIM)
    scores = jnp.where(live_mask[None, None, :], scores, -1e30)
    new_max = jnp.maximum(running_max, jnp.max(scores, axis=2))
    weights = jnp.where(live_mask[None, None, :], jnp.exp(scores - new_max[:, :, None]), 0.0)
    factor = jnp.exp(running_max - new_max)
    row_total = row_total * factor + jnp.sum(weights, axis=2)
    weighted_sum = weighted_sum * factor[:, :, None] + jnp.einsum(
        "pqk,kpd->pqd", weights.astype(jnp.bfloat16), value_rows, preferred_element_type=jnp.float32
    )
    return (new_max, row_total, weighted_sum)


def empty_state(head_count, query_count):
    return (
        jnp.full((head_count, query_count), -1e30, jnp.float32),
        jnp.zeros((head_count, query_count), jnp.float32),
        jnp.zeros((head_count, query_count, HEAD_DIM), jnp.float32),
    )


def finish(run_state):
    running_max, row_total, weighted_sum = run_state
    return (weighted_sum / row_total[:, :, None]).transpose(1, 0, 2).astype(jnp.bfloat16)


def block_attention(queries, key_rows, value_rows, live_mask):
    query_total, heads_here, head_width = queries.shape
    key_total = key_rows.shape[0]
    key_block = 1024 if key_total % 1024 == 0 else key_total
    query_block = 512 if query_total % 512 == 0 else query_total
    key_blocks = key_rows.reshape(key_total // key_block, key_block, heads_here, head_width)
    value_blocks = value_rows.reshape(key_total // key_block, key_block, heads_here, head_width)
    live_blocks = live_mask.reshape(key_total // key_block, key_block)

    def one_block(query_piece):

        def absorb_block(run_state, pieces):
            return (absorb(run_state, query_piece, pieces[0], pieces[1], pieces[2]), None)

        final_state, unused = lax.scan(
            absorb_block,
            empty_state(heads_here, query_block),
            (key_blocks, value_blocks, live_blocks),
        )
        return finish(final_state)

    blended = lax.map(
        one_block, queries.reshape(query_total // query_block, query_block, heads_here, head_width)
    )
    return blended.reshape(query_total, heads_here, head_width)


def shards(self_queries, self_keys, self_values, text_queries, text_kv, text_len):
    token_rows = self_queries.shape[1]
    channel_count = self_queries.shape[2]
    seq_count = lax.axis_size("seq")
    quarter_count = max(seq_count // HEADS, 1)
    heads_here = max(HEADS // seq_count, 1)
    group_count = HEADS // heads_here
    head_span = heads_here * HEAD_DIM
    share_rows = token_rows // quarter_count
    query_total = share_rows * seq_count
    branch = lax.axis_index("enc")
    length = lax.dynamic_index_in_dim(text_len, branch, 0, keepdims=False)

    def head_view(tensor):
        return tensor.reshape(1, share_rows, seq_count, head_span)

    def repeated(tensor):
        spread = jnp.broadcast_to(
            tensor.reshape(1, token_rows, 1, group_count, head_span),
            (1, token_rows, quarter_count, group_count, head_span),
        )
        return spread.reshape(1, token_rows, seq_count, head_span)

    head_queries, head_keys, head_values = (
        lax.all_to_all(head_view(self_queries), "seq", split_axis=2, concat_axis=1, tiled=True),
        lax.all_to_all(repeated(self_keys), "seq", split_axis=2, concat_axis=1, tiled=True),
        lax.all_to_all(repeated(self_values), "seq", split_axis=2, concat_axis=1, tiled=True),
    )
    key_rows = head_keys.reshape(-1, heads_here, HEAD_DIM)
    value_rows = head_values.reshape(-1, heads_here, HEAD_DIM)
    query_rows = head_queries.reshape(query_total, heads_here, HEAD_DIM)
    every_key = jnp.ones((key_rows.shape[0],), jnp.bool_)
    self_heads = block_attention(query_rows, key_rows, value_rows, every_key)
    head_text_queries = lax.all_to_all(
        head_view(text_queries), "seq", split_axis=2, concat_axis=1, tiled=True
    )
    context_rows = text_kv.shape[2]
    spread = jnp.broadcast_to(
        text_kv.reshape(1, 2, context_rows, 1, group_count, head_span),
        (1, 2, context_rows, quarter_count, group_count, head_span),
    )
    head_context = lax.all_to_all(
        spread.reshape(1, 2, context_rows, seq_count, head_span),
        "seq",
        split_axis=3,
        concat_axis=2,
        tiled=True,
    )
    text_total = head_context.shape[2]
    context_keys = head_context[0, 0].reshape(text_total, heads_here, HEAD_DIM)
    context_values = head_context[0, 1].reshape(text_total, heads_here, HEAD_DIM)
    live_mask = jnp.arange(text_total, dtype=jnp.int32) < length
    text_heads = block_attention(
        head_text_queries.reshape(query_total, heads_here, HEAD_DIM),
        context_keys,
        context_values,
        live_mask,
    )
    self_view = self_heads.reshape(1, seq_count, share_rows, 1, head_span)
    text_view = text_heads.reshape(1, seq_count, share_rows, 1, head_span)
    self_back, text_back = (
        lax.all_to_all(self_view, "seq", split_axis=1, concat_axis=3, tiled=True),
        lax.all_to_all(text_view, "seq", split_axis=1, concat_axis=3, tiled=True),
    )
    self_mixed = self_back.reshape(1, token_rows, channel_count)
    text_mixed = text_back.reshape(1, token_rows, channel_count)
    return (self_mixed, text_mixed)


HALVES = 2
MESH = pl.DeviceIdType.MESH
FAR = -1e30


def attend(queries, key_rows, value_rows, live):
    scores = lax.dot_general(
        queries, key_rows, (((1,), (1,)), ((), ())), preferred_element_type=jnp.float32
    ) * (1.0 / math.sqrt(HEAD_DIM))
    if live is not None:
        scores = jnp.where(live, scores, FAR)
    top = jnp.max(scores, axis=1, keepdims=True)
    weights = jnp.exp(scores - top)
    if live is not None:
        weights = jnp.where(live, weights, 0.0)
    total = jnp.sum(weights, axis=1, keepdims=True)
    mixed = jnp.dot(weights.astype(jnp.bfloat16), value_rows, preferred_element_type=jnp.float32)
    return mixed, top, total


def fused(
    count,
    self_q,
    self_k,
    self_v,
    text_q,
    text_kv,
    text_len,
    self_out,
    text_out,
    own_q,
    own_k,
    own_v,
    text_rows,
    context,
    self_part,
    text_part,
    stat_part,
    text_back,
    stat_back,
    send_sem,
    recv_sem,
    local_sem,
):
    me = lax.axis_index("seq")
    branch = lax.axis_index("enc")
    ring = count // HALVES
    half, place = lax.div(me, ring), lax.rem(me, ring)
    rows = self_q.shape[1]
    query_total = count * rows
    context_rows = text_kv.shape[2]
    key_total = ring * context_rows
    self_span = own_q.shape[2]
    text_span = text_rows.shape[2]
    self_heads, text_heads = self_span // HEAD_DIM, text_span // HEAD_DIM

    def peer(step):
        return lax.rem(me + step, count)

    def near(step):
        return half * ring + lax.rem(place + step, ring)

    def self_cols(device):
        return pl.ds(pl.multiple_of(device * self_span, self_span), self_span)

    def text_cols(device):
        return pl.ds(pl.multiple_of(lax.rem(device, ring) * text_span, text_span), text_span)

    def remote(kind, step, source, target, device):
        return pltpu.make_async_remote_copy(
            src_ref=source,
            dst_ref=target,
            send_sem=send_sem.at[kind, step],
            recv_sem=recv_sem.at[kind, step],
            device_id={"seq": device},
            device_id_type=MESH,
        )

    kept = [
        pltpu.make_async_copy(text_q.at[0, :, text_cols(me)], text_rows.at[me], local_sem.at[0]),
        pltpu.make_async_copy(text_kv.at[0, :, :, text_cols(me)], context.at[place], local_sem.at[1]),
        pltpu.make_async_copy(self_q.at[0, :, self_cols(me)], own_q.at[me], local_sem.at[2]),
        pltpu.make_async_copy(self_k.at[0, :, self_cols(me)], own_k.at[me], local_sem.at[3]),
        pltpu.make_async_copy(self_v.at[0, :, self_cols(me)], own_v.at[me], local_sem.at[4]),
    ]
    for copy in kept:
        copy.start()

    barrier = pltpu.get_barrier_semaphore()
    for step in range(1, count):
        pl.semaphore_signal(barrier, inc=1, device_id={"seq": peer(step)}, device_id_type=MESH)
    pl.semaphore_wait(barrier, count - 1)

    text_in, self_in = [], []
    for step in range(1, count):
        to = peer(step)
        text_in.append(remote(0, step, text_q.at[0, :, text_cols(to)], text_rows.at[me], to))
    for step in range(1, ring):
        to = near(step)
        text_in.append(remote(1, step, text_kv.at[0, :, :, text_cols(to)], context.at[place], to))
    for kind, source, target in ((2, self_q, own_q), (3, self_k, own_k), (4, self_v, own_v)):
        for step in range(1, count):
            to = peer(step)
            self_in.append(remote(kind, step, source.at[0, :, self_cols(to)], target.at[me], to))
    for copy in text_in + self_in:
        copy.start()

    for copy in kept[:2]:
        copy.wait()
    for copy in text_in:
        copy.wait_recv()
    length = text_len[branch]
    live = half * key_total + lax.broadcasted_iota(jnp.int32, (1, key_total), 1) < length
    lane = lax.broadcasted_iota(jnp.int32, (query_total, HEAD_DIM), 1)
    stats = jnp.full((query_total, HEAD_DIM), FAR, jnp.float32)
    for head in range(text_heads):
        span = slice(head * HEAD_DIM, (head + 1) * HEAD_DIM)
        mixed, top, total = attend(
            text_rows[:, :, span].reshape(query_total, HEAD_DIM),
            context[:, 0, :, span].reshape(key_total, HEAD_DIM),
            context[:, 1, :, span].reshape(key_total, HEAD_DIM),
            live,
        )
        safe = jnp.where(total > 0.0, total, 1.0)
        weight = jnp.where(total > 0.0, top + jnp.log(safe), FAR)
        text_part[:, :, span] = (mixed / safe).astype(jnp.bfloat16).reshape(count, rows, HEAD_DIM)
        stats = jnp.where(lane == head, weight, stats)
    stat_part[...] = stats.reshape(count, rows, HEAD_DIM)
    kept.append(pltpu.make_async_copy(text_part.at[me], text_back.at[half, :, text_cols(me)], local_sem.at[5]))
    kept.append(pltpu.make_async_copy(stat_part.at[me], stat_back.at[me], local_sem.at[6]))
    kept[5].start()
    kept[6].start()
    text_return = []
    for step in range(1, count):
        to = peer(step)
        text_return.append(remote(6, step, stat_part.at[to], stat_back.at[me], to))
        text_return.append(remote(5, step, text_part.at[to], text_back.at[half, :, text_cols(me)], to))
    for copy in text_return:
        copy.start()

    for copy in kept[2:5]:
        copy.wait()
    for copy in self_in:
        copy.wait_recv()
    for head in range(self_heads):
        span = slice(head * HEAD_DIM, (head + 1) * HEAD_DIM)
        mixed, top, total = attend(
            own_q[:, :, span].reshape(query_total, HEAD_DIM),
            own_k[:, :, span].reshape(query_total, HEAD_DIM),
            own_v[:, :, span].reshape(query_total, HEAD_DIM),
            None,
        )
        self_part[:, :, span] = (mixed / total).astype(jnp.bfloat16).reshape(count, rows, HEAD_DIM)
    kept.append(pltpu.make_async_copy(self_part.at[me], self_out.at[0, :, self_cols(me)], local_sem.at[7]))
    kept[7].start()
    self_return = []
    for step in range(1, count):
        to = peer(step)
        self_return.append(remote(7, step, self_part.at[to], self_out.at[0, :, self_cols(me)], to))
    for copy in self_return:
        copy.start()

    kept[5].wait()
    kept[6].wait()
    for copy in text_return:
        copy.wait_recv()
    for group in range(ring):
        sides = [stat_back[side * ring + group] for side in range(HALVES)]
        highest = functools.reduce(jnp.maximum, sides)
        shares = [jnp.exp(side - highest) for side in sides]
        whole = sum(shares)
        shares = [share / whole for share in shares]
        for head in range(text_heads):
            start = group * text_span + head * HEAD_DIM
            span = slice(start, start + HEAD_DIM)
            merged = sum(
                text_back[side, :, span].astype(jnp.float32) * shares[side][:, head : head + 1]
                for side in range(HALVES)
            )
            text_out[0, :, span] = merged.astype(jnp.bfloat16)

    kept[7].wait()
    for copy in self_return:
        copy.wait_recv()
    for copy in text_in + self_in + text_return + self_return:
        copy.wait_send()


def fused_shards(self_queries, self_keys, self_values, text_queries, text_kv, text_len):
    count = lax.axis_size("seq")
    rows, channels = self_queries.shape[1:]
    context_rows = text_kv.shape[2]
    ring = count // HALVES
    self_span, text_span = channels // count, channels // ring
    in_place = pl.BlockSpec(memory_space=pl.ANY)
    bf16, f32 = jnp.bfloat16, jnp.float32
    out = jax.ShapeDtypeStruct((1, rows, channels), bf16)
    return pl.pallas_call(
        functools.partial(fused, count),
        out_shape=(out, out),
        in_specs=[in_place] * 5 + [pl.BlockSpec(memory_space=pltpu.SMEM)],
        out_specs=(in_place, pl.BlockSpec(memory_space=pltpu.VMEM)),
        scratch_shapes=[
            pltpu.VMEM((count, rows, self_span), bf16),
            pltpu.VMEM((count, rows, self_span), bf16),
            pltpu.VMEM((count, rows, self_span), bf16),
            pltpu.VMEM((count, rows, text_span), bf16),
            pltpu.VMEM((ring, 2, context_rows, text_span), bf16),
            pltpu.VMEM((count, rows, self_span), bf16),
            pltpu.VMEM((count, rows, text_span), bf16),
            pltpu.VMEM((count, rows, HEAD_DIM), f32),
            pltpu.VMEM((HALVES, rows, channels), bf16),
            pltpu.VMEM((count, rows, HEAD_DIM), f32),
            pltpu.SemaphoreType.DMA((8, count)),
            pltpu.SemaphoreType.DMA((8, count)),
            pltpu.SemaphoreType.DMA((8,)),
        ],
        compiler_params=pltpu.CompilerParams(collective_id=0, has_side_effects=True),
        name="attention",
    )(self_queries, self_keys, self_values, text_queries, text_kv, text_len)


def solution(mesh):
    count = mesh.shape["seq"]
    fits = count % HALVES == 0 and HEADS % count == 0
    return jax.shard_map(
        fused_shards if fits else shards,
        mesh=mesh,
        in_specs=(
            P("enc", ("groups", "seq"), None),
            P("enc", ("groups", "seq"), None),
            P("enc", ("groups", "seq"), None),
            P("enc", ("groups", "seq"), None),
            P("enc", None, ("groups", "seq"), None),
            P("groups"),
        ),
        out_specs=(P("enc", ("groups", "seq"), None), P("enc", ("groups", "seq"), None)),
        check_vma=False,
    )
```

```python
import functools
import math

import jax
import jax.numpy as jnp
from jax import lax
from jax.experimental import pallas as pl
from jax.experimental.pallas import tpu as pltpu
from jax.sharding import PartitionSpec as P

HEADS = 32
HEAD_DIM = 128


def absorb(run_state, queries, key_rows, value_rows, live_mask):
    running_max, row_total, weighted_sum = run_state
    scores = jnp.einsum(
        "qpd,kpd->pqk", queries, key_rows, preferred_element_type=jnp.float32
    ) / math.sqrt(HEAD_DIM)
    scores = jnp.where(live_mask[None, None, :], scores, -1e30)
    new_max = jnp.maximum(running_max, jnp.max(scores, axis=2))
    weights = jnp.where(live_mask[None, None, :], jnp.exp(scores - new_max[:, :, None]), 0.0)
    factor = jnp.exp(running_max - new_max)
    row_total = row_total * factor + jnp.sum(weights, axis=2)
    weighted_sum = weighted_sum * factor[:, :, None] + jnp.einsum(
        "pqk,kpd->pqd", weights.astype(jnp.bfloat16), value_rows, preferred_element_type=jnp.float32
    )
    return (new_max, row_total, weighted_sum)


def empty_state(head_count, query_count):
    return (
        jnp.full((head_count, query_count), -1e30, jnp.float32),
        jnp.zeros((head_count, query_count), jnp.float32),
        jnp.zeros((head_count, query_count, HEAD_DIM), jnp.float32),
    )


def finish(run_state):
    running_max, row_total, weighted_sum = run_state
    return (weighted_sum / row_total[:, :, None]).transpose(1, 0, 2).astype(jnp.bfloat16)


def block_attention(queries, key_rows, value_rows, live_mask):
    query_total, heads_here, head_width = queries.shape
    key_total = key_rows.shape[0]
    key_block = 1024 if key_total % 1024 == 0 else key_total
    query_block = 512 if query_total % 512 == 0 else query_total
    key_blocks = key_rows.reshape(key_total // key_block, key_block, heads_here, head_width)
    value_blocks = value_rows.reshape(key_total // key_block, key_block, heads_here, head_width)
    live_blocks = live_mask.reshape(key_total // key_block, key_block)

    def one_block(query_piece):

        def absorb_block(run_state, pieces):
            return (absorb(run_state, query_piece, pieces[0], pieces[1], pieces[2]), None)

        final_state, unused = lax.scan(
            absorb_block,
            empty_state(heads_here, query_block),
            (key_blocks, value_blocks, live_blocks),
        )
        return finish(final_state)

    blended = lax.map(
        one_block, queries.reshape(query_total // query_block, query_block, heads_here, head_width)
    )
    return blended.reshape(query_total, heads_here, head_width)


def shards(self_queries, self_keys, self_values, text_queries, text_kv, text_len):
    token_rows = self_queries.shape[1]
    channel_count = self_queries.shape[2]
    seq_count = lax.axis_size("seq")
    quarter_count = max(seq_count // HEADS, 1)
    heads_here = max(HEADS // seq_count, 1)
    group_count = HEADS // heads_here
    head_span = heads_here * HEAD_DIM
    share_rows = token_rows // quarter_count
    query_total = share_rows * seq_count
    branch = lax.axis_index("enc")
    length = lax.dynamic_index_in_dim(text_len, branch, 0, keepdims=False)

    def head_view(tensor):
        return tensor.reshape(1, share_rows, seq_count, head_span)

    def repeated(tensor):
        spread = jnp.broadcast_to(
            tensor.reshape(1, token_rows, 1, group_count, head_span),
            (1, token_rows, quarter_count, group_count, head_span),
        )
        return spread.reshape(1, token_rows, seq_count, head_span)

    head_queries, head_keys, head_values = (
        lax.all_to_all(head_view(self_queries), "seq", split_axis=2, concat_axis=1, tiled=True),
        lax.all_to_all(repeated(self_keys), "seq", split_axis=2, concat_axis=1, tiled=True),
        lax.all_to_all(repeated(self_values), "seq", split_axis=2, concat_axis=1, tiled=True),
    )
    key_rows = head_keys.reshape(-1, heads_here, HEAD_DIM)
    value_rows = head_values.reshape(-1, heads_here, HEAD_DIM)
    query_rows = head_queries.reshape(query_total, heads_here, HEAD_DIM)
    every_key = jnp.ones((key_rows.shape[0],), jnp.bool_)
    self_heads = block_attention(query_rows, key_rows, value_rows, every_key)
    head_text_queries = lax.all_to_all(
        head_view(text_queries), "seq", split_axis=2, concat_axis=1, tiled=True
    )
    context_rows = text_kv.shape[2]
    spread = jnp.broadcast_to(
        text_kv.reshape(1, 2, context_rows, 1, group_count, head_span),
        (1, 2, context_rows, quarter_count, group_count, head_span),
    )
    head_context = lax.all_to_all(
        spread.reshape(1, 2, context_rows, seq_count, head_span),
        "seq",
        split_axis=3,
        concat_axis=2,
        tiled=True,
    )
    text_total = head_context.shape[2]
    context_keys = head_context[0, 0].reshape(text_total, heads_here, HEAD_DIM)
    context_values = head_context[0, 1].reshape(text_total, heads_here, HEAD_DIM)
    live_mask = jnp.arange(text_total, dtype=jnp.int32) < length
    text_heads = block_attention(
        head_text_queries.reshape(query_total, heads_here, HEAD_DIM),
        context_keys,
        context_values,
        live_mask,
    )
    self_view = self_heads.reshape(1, seq_count, share_rows, 1, head_span)
    text_view = text_heads.reshape(1, seq_count, share_rows, 1, head_span)
    self_back, text_back = (
        lax.all_to_all(self_view, "seq", split_axis=1, concat_axis=3, tiled=True),
        lax.all_to_all(text_view, "seq", split_axis=1, concat_axis=3, tiled=True),
    )
    self_mixed = self_back.reshape(1, token_rows, channel_count)
    text_mixed = text_back.reshape(1, token_rows, channel_count)
    return (self_mixed, text_mixed)


HALVES = 2
MESH = pl.DeviceIdType.MESH
FAR = -1e30


def attend(queries, key_rows, value_rows, live):
    scores = lax.dot_general(
        queries, key_rows, (((1,), (1,)), ((), ())), preferred_element_type=jnp.float32
    ) * (1.0 / math.sqrt(HEAD_DIM))
    if live is not None:
        scores = jnp.where(live, scores, FAR)
    top = jnp.max(scores, axis=1, keepdims=True)
    weights = jnp.exp(scores - top)
    if live is not None:
        weights = jnp.where(live, weights, 0.0)
    total = jnp.sum(weights, axis=1, keepdims=True)
    mixed = jnp.dot(weights.astype(jnp.bfloat16), value_rows, preferred_element_type=jnp.float32)
    return mixed, top, total


def fused(
    count,
    self_q,
    self_k,
    self_v,
    text_q,
    text_kv,
    text_len,
    self_out,
    text_out,
    own_q,
    own_k,
    own_v,
    text_rows,
    context,
    self_part,
    text_part,
    stat_part,
    text_back,
    stat_back,
    stat_cols,
    send_sem,
    recv_sem,
    local_sem,
):
    me = lax.axis_index("seq")
    branch = lax.axis_index("enc")
    ring = count // HALVES
    half, place = lax.div(me, ring), lax.rem(me, ring)
    rows = self_q.shape[1]
    query_total = count * rows
    context_rows = text_kv.shape[2]
    key_total = ring * context_rows
    self_span = own_q.shape[2]
    text_span = text_rows.shape[2]
    self_heads, text_heads = self_span // HEAD_DIM, text_span // HEAD_DIM

    def peer(step):
        return lax.rem(me + step, count)

    def near(step):
        return half * ring + lax.rem(place + step, ring)

    def self_cols(device):
        return pl.ds(pl.multiple_of(device * self_span, self_span), self_span)

    def text_cols(device):
        return pl.ds(pl.multiple_of(lax.rem(device, ring) * text_span, text_span), text_span)

    def remote(kind, step, source, target, device):
        return pltpu.make_async_remote_copy(
            src_ref=source,
            dst_ref=target,
            send_sem=send_sem.at[kind, step],
            recv_sem=recv_sem.at[kind, step],
            device_id={"seq": device},
            device_id_type=MESH,
        )

    kept = [
        pltpu.make_async_copy(text_q.at[0, :, text_cols(me)], text_rows.at[me], local_sem.at[0]),
        pltpu.make_async_copy(text_kv.at[0, :, :, text_cols(me)], context.at[place], local_sem.at[1]),
        pltpu.make_async_copy(self_q.at[0, :, self_cols(me)], own_q.at[me], local_sem.at[2]),
        pltpu.make_async_copy(self_k.at[0, :, self_cols(me)], own_k.at[me], local_sem.at[3]),
        pltpu.make_async_copy(self_v.at[0, :, self_cols(me)], own_v.at[me], local_sem.at[4]),
    ]
    for copy in kept:
        copy.start()

    barrier = pltpu.get_barrier_semaphore()
    for step in range(1, count):
        pl.semaphore_signal(barrier, inc=1, device_id={"seq": peer(step)}, device_id_type=MESH)
    pl.semaphore_wait(barrier, count - 1)

    text_in, self_in = [], []
    for step in range(1, count):
        to = peer(step)
        text_in.append(remote(0, step, text_q.at[0, :, text_cols(to)], text_rows.at[me], to))
    for step in range(1, ring):
        to = near(step)
        text_in.append(remote(1, step, text_kv.at[0, :, :, text_cols(to)], context.at[place], to))
    for kind, source, target in ((2, self_q, own_q), (3, self_k, own_k), (4, self_v, own_v)):
        for step in range(1, count):
            to = peer(step)
            self_in.append(remote(kind, step, source.at[0, :, self_cols(to)], target.at[me], to))
    for copy in text_in + self_in:
        copy.start()

    for copy in kept[:2]:
        copy.wait()
    for copy in text_in:
        copy.wait_recv()
    length = text_len[branch]
    live = half * key_total + lax.broadcasted_iota(jnp.int32, (1, key_total), 1) < length
    lane = lax.broadcasted_iota(jnp.int32, (query_total, HEAD_DIM), 1)
    stats = jnp.full((query_total, HEAD_DIM), FAR, jnp.float32)
    for head in range(text_heads):
        span = slice(head * HEAD_DIM, (head + 1) * HEAD_DIM)
        mixed, top, total = attend(
            text_rows[:, :, span].reshape(query_total, HEAD_DIM),
            context[:, 0, :, span].reshape(key_total, HEAD_DIM),
            context[:, 1, :, span].reshape(key_total, HEAD_DIM),
            live,
        )
        safe = jnp.where(total > 0.0, total, 1.0)
        weight = jnp.where(total > 0.0, top + jnp.log(safe), FAR)
        text_part[:, :, span] = (mixed / safe).astype(jnp.bfloat16).reshape(count, rows, HEAD_DIM)
        stats = jnp.where(lane == head, weight, stats)
    stat_part[...] = stats.T[:text_heads]
    kept.append(pltpu.make_async_copy(text_part.at[me], text_back.at[half, :, text_cols(me)], local_sem.at[5]))
    kept.append(pltpu.make_async_copy(stat_part, stat_back.at[me], local_sem.at[6]))
    kept[5].start()
    kept[6].start()
    text_return = []
    for step in range(1, count):
        to = peer(step)
        text_return.append(remote(6, step, stat_part, stat_back.at[me], to))
        text_return.append(remote(5, step, text_part.at[to], text_back.at[half, :, text_cols(me)], to))
    for copy in text_return:
        copy.start()

    for copy in kept[2:5]:
        copy.wait()
    for copy in self_in:
        copy.wait_recv()
    for head in range(self_heads):
        span = slice(head * HEAD_DIM, (head + 1) * HEAD_DIM)
        mixed, top, total = attend(
            own_q[:, :, span].reshape(query_total, HEAD_DIM),
            own_k[:, :, span].reshape(query_total, HEAD_DIM),
            own_v[:, :, span].reshape(query_total, HEAD_DIM),
            None,
        )
        self_part[:, :, span] = (mixed / total).astype(jnp.bfloat16).reshape(count, rows, HEAD_DIM)
    kept.append(pltpu.make_async_copy(self_part.at[me], self_out.at[0, :, self_cols(me)], local_sem.at[7]))
    kept[7].start()
    self_return = []
    for step in range(1, count):
        to = peer(step)
        self_return.append(remote(7, step, self_part.at[to], self_out.at[0, :, self_cols(me)], to))
    for copy in self_return:
        copy.start()

    kept[5].wait()
    kept[6].wait()
    for copy in text_return:
        copy.wait_recv()
    stat_cols[...] = stat_back[...].reshape(HALVES * HEADS, query_total).T
    mine = stat_cols[pl.ds(pl.multiple_of(me * rows, rows), rows), :]
    sides = [mine[:, side * HEADS : (side + 1) * HEADS] for side in range(HALVES)]
    highest = functools.reduce(jnp.maximum, sides)
    shares = [jnp.exp(side - highest) for side in sides]
    whole = sum(shares)
    shares = [share / whole for share in shares]
    for head in range(HEADS):
        span = slice(head * HEAD_DIM, (head + 1) * HEAD_DIM)
        merged = sum(
            text_back[side, :, span].astype(jnp.float32) * shares[side][:, head : head + 1]
            for side in range(HALVES)
        )
        text_out[0, :, span] = merged.astype(jnp.bfloat16)

    kept[7].wait()
    for copy in self_return:
        copy.wait_recv()
    for copy in text_in + self_in + text_return + self_return:
        copy.wait_send()


def carry(*refs):
    sources, targets, held, sem = refs[0:2], refs[2:4], refs[4:6], refs[6]
    steps = []
    for n in range(2):
        steps.append(pltpu.make_async_copy(sources[n], held[n], sem.at[0, n]))
        steps[n].start()
    ends = []
    for n in range(2):
        steps[n].wait()
        ends.append(pltpu.make_async_copy(held[n], targets[n], sem.at[1, n]))
        ends[n].start()
    for end in ends:
        end.wait()


def fused_shards(self_queries, self_keys, self_values, text_queries, text_kv, text_len):
    count = lax.axis_size("seq")
    rows, channels = self_queries.shape[1:]
    context_rows = text_kv.shape[2]
    ring = count // HALVES
    self_span, text_span = channels // count, channels // ring
    in_place = pl.BlockSpec(memory_space=pl.ANY)
    bf16, f32 = jnp.bfloat16, jnp.float32
    out = jax.ShapeDtypeStruct((1, rows, channels), bf16)
    results = pl.pallas_call(
        functools.partial(fused, count),
        out_shape=(out, out),
        in_specs=[in_place] * 5 + [pl.BlockSpec(memory_space=pltpu.SMEM)],
        out_specs=(in_place, pl.BlockSpec(memory_space=pltpu.VMEM)),
        scratch_shapes=[
            pltpu.VMEM((count, rows, self_span), bf16),
            pltpu.VMEM((count, rows, self_span), bf16),
            pltpu.VMEM((count, rows, self_span), bf16),
            pltpu.VMEM((count, rows, text_span), bf16),
            pltpu.VMEM((ring, 2, context_rows, text_span), bf16),
            pltpu.VMEM((count, rows, self_span), bf16),
            pltpu.VMEM((count, rows, text_span), bf16),
            pltpu.VMEM((text_span // HEAD_DIM, count * rows), f32),
            pltpu.VMEM((HALVES, rows, channels), bf16),
            pltpu.VMEM((count, text_span // HEAD_DIM, count * rows), f32),
            pltpu.VMEM((count * rows, HALVES * HEADS), f32),
            pltpu.SemaphoreType.DMA((8, count)),
            pltpu.SemaphoreType.DMA((8, count)),
            pltpu.SemaphoreType.DMA((8,)),
        ],
        compiler_params=pltpu.CompilerParams(collective_id=0, has_side_effects=True),
        name="attention",
    )(self_queries, self_keys, self_values, text_queries, text_kv, text_len)
    return pl.pallas_call(
        carry,
        out_shape=(out, out),
        in_specs=[in_place] * 2,
        out_specs=(in_place, in_place),
        scratch_shapes=[
            pltpu.VMEM((1, rows, channels), bf16),
            pltpu.VMEM((1, rows, channels), bf16),
            pltpu.SemaphoreType.DMA((2, 2)),
        ],
        name="carry",
    )(*results)


def solution(mesh):
    count = mesh.shape["seq"]
    fits = count % HALVES == 0 and HEADS % count == 0
    return jax.shard_map(
        fused_shards if fits else shards,
        mesh=mesh,
        in_specs=(
            P("enc", ("groups", "seq"), None),
            P("enc", ("groups", "seq"), None),
            P("enc", ("groups", "seq"), None),
            P("enc", ("groups", "seq"), None),
            P("enc", None, ("groups", "seq"), None),
            P("groups"),
        ),
        out_specs=(P("enc", ("groups", "seq"), None), P("enc", ("groups", "seq"), None)),
        check_vma=False,
    )
```

```python
import functools
import math

import jax
import jax.numpy as jnp
from jax import lax
from jax.experimental import pallas as pl
from jax.experimental.pallas import tpu as pltpu
from jax.sharding import PartitionSpec as P

HEADS = 32
HEAD_DIM = 128


def absorb(run_state, queries, key_rows, value_rows, live_mask):
    running_max, row_total, weighted_sum = run_state
    scores = jnp.einsum(
        "qpd,kpd->pqk", queries, key_rows, preferred_element_type=jnp.float32
    ) / math.sqrt(HEAD_DIM)
    scores = jnp.where(live_mask[None, None, :], scores, -1e30)
    new_max = jnp.maximum(running_max, jnp.max(scores, axis=2))
    weights = jnp.where(live_mask[None, None, :], jnp.exp(scores - new_max[:, :, None]), 0.0)
    factor = jnp.exp(running_max - new_max)
    row_total = row_total * factor + jnp.sum(weights, axis=2)
    weighted_sum = weighted_sum * factor[:, :, None] + jnp.einsum(
        "pqk,kpd->pqd", weights.astype(jnp.bfloat16), value_rows, preferred_element_type=jnp.float32
    )
    return (new_max, row_total, weighted_sum)


def empty_state(head_count, query_count):
    return (
        jnp.full((head_count, query_count), -1e30, jnp.float32),
        jnp.zeros((head_count, query_count), jnp.float32),
        jnp.zeros((head_count, query_count, HEAD_DIM), jnp.float32),
    )


def finish(run_state):
    running_max, row_total, weighted_sum = run_state
    return (weighted_sum / row_total[:, :, None]).transpose(1, 0, 2).astype(jnp.bfloat16)


def block_attention(queries, key_rows, value_rows, live_mask):
    query_total, heads_here, head_width = queries.shape
    key_total = key_rows.shape[0]
    key_block = 1024 if key_total % 1024 == 0 else key_total
    query_block = 512 if query_total % 512 == 0 else query_total
    key_blocks = key_rows.reshape(key_total // key_block, key_block, heads_here, head_width)
    value_blocks = value_rows.reshape(key_total // key_block, key_block, heads_here, head_width)
    live_blocks = live_mask.reshape(key_total // key_block, key_block)

    def one_block(query_piece):

        def absorb_block(run_state, pieces):
            return (absorb(run_state, query_piece, pieces[0], pieces[1], pieces[2]), None)

        final_state, unused = lax.scan(
            absorb_block,
            empty_state(heads_here, query_block),
            (key_blocks, value_blocks, live_blocks),
        )
        return finish(final_state)

    blended = lax.map(
        one_block, queries.reshape(query_total // query_block, query_block, heads_here, head_width)
    )
    return blended.reshape(query_total, heads_here, head_width)


def shards(self_queries, self_keys, self_values, text_queries, text_kv, text_len):
    token_rows = self_queries.shape[1]
    channel_count = self_queries.shape[2]
    seq_count = lax.axis_size("seq")
    quarter_count = max(seq_count // HEADS, 1)
    heads_here = max(HEADS // seq_count, 1)
    group_count = HEADS // heads_here
    head_span = heads_here * HEAD_DIM
    share_rows = token_rows // quarter_count
    query_total = share_rows * seq_count
    branch = lax.axis_index("enc")
    length = lax.dynamic_index_in_dim(text_len, branch, 0, keepdims=False)

    def head_view(tensor):
        return tensor.reshape(1, share_rows, seq_count, head_span)

    def repeated(tensor):
        spread = jnp.broadcast_to(
            tensor.reshape(1, token_rows, 1, group_count, head_span),
            (1, token_rows, quarter_count, group_count, head_span),
        )
        return spread.reshape(1, token_rows, seq_count, head_span)

    head_queries, head_keys, head_values = (
        lax.all_to_all(head_view(self_queries), "seq", split_axis=2, concat_axis=1, tiled=True),
        lax.all_to_all(repeated(self_keys), "seq", split_axis=2, concat_axis=1, tiled=True),
        lax.all_to_all(repeated(self_values), "seq", split_axis=2, concat_axis=1, tiled=True),
    )
    key_rows = head_keys.reshape(-1, heads_here, HEAD_DIM)
    value_rows = head_values.reshape(-1, heads_here, HEAD_DIM)
    query_rows = head_queries.reshape(query_total, heads_here, HEAD_DIM)
    every_key = jnp.ones((key_rows.shape[0],), jnp.bool_)
    self_heads = block_attention(query_rows, key_rows, value_rows, every_key)
    head_text_queries = lax.all_to_all(
        head_view(text_queries), "seq", split_axis=2, concat_axis=1, tiled=True
    )
    context_rows = text_kv.shape[2]
    spread = jnp.broadcast_to(
        text_kv.reshape(1, 2, context_rows, 1, group_count, head_span),
        (1, 2, context_rows, quarter_count, group_count, head_span),
    )
    head_context = lax.all_to_all(
        spread.reshape(1, 2, context_rows, seq_count, head_span),
        "seq",
        split_axis=3,
        concat_axis=2,
        tiled=True,
    )
    text_total = head_context.shape[2]
    context_keys = head_context[0, 0].reshape(text_total, heads_here, HEAD_DIM)
    context_values = head_context[0, 1].reshape(text_total, heads_here, HEAD_DIM)
    live_mask = jnp.arange(text_total, dtype=jnp.int32) < length
    text_heads = block_attention(
        head_text_queries.reshape(query_total, heads_here, HEAD_DIM),
        context_keys,
        context_values,
        live_mask,
    )
    self_view = self_heads.reshape(1, seq_count, share_rows, 1, head_span)
    text_view = text_heads.reshape(1, seq_count, share_rows, 1, head_span)
    self_back, text_back = (
        lax.all_to_all(self_view, "seq", split_axis=1, concat_axis=3, tiled=True),
        lax.all_to_all(text_view, "seq", split_axis=1, concat_axis=3, tiled=True),
    )
    self_mixed = self_back.reshape(1, token_rows, channel_count)
    text_mixed = text_back.reshape(1, token_rows, channel_count)
    return (self_mixed, text_mixed)


HALVES = 2
MESH = pl.DeviceIdType.MESH
FAR = -1e30


def attend(queries, key_rows, value_rows, live):
    scores = lax.dot_general(
        queries, key_rows, (((1,), (1,)), ((), ())), preferred_element_type=jnp.float32
    ) * (1.0 / math.sqrt(HEAD_DIM))
    if live is not None:
        scores = jnp.where(live, scores, FAR)
    top = jnp.max(scores, axis=1, keepdims=True)
    weights = jnp.exp(scores - top)
    if live is not None:
        weights = jnp.where(live, weights, 0.0)
    total = jnp.sum(weights, axis=1, keepdims=True)
    mixed = jnp.dot(weights.astype(jnp.bfloat16), value_rows, preferred_element_type=jnp.float32)
    return mixed, top, total


def fused(
    count,
    self_q,
    self_k,
    self_v,
    text_q,
    text_kv,
    text_len,
    self_out,
    text_out,
    own_q,
    own_k,
    own_v,
    text_rows,
    context,
    self_part,
    text_part,
    stat_part,
    text_back,
    stat_back,
    stat_cols,
    send_sem,
    recv_sem,
    local_sem,
):
    me = lax.axis_index("seq")
    branch = lax.axis_index("enc")
    ring = count // HALVES
    half, place = lax.div(me, ring), lax.rem(me, ring)
    rows = self_q.shape[1]
    query_total = count * rows
    context_rows = text_kv.shape[2]
    key_total = ring * context_rows
    self_span = own_q.shape[2]
    text_span = text_rows.shape[2]
    self_heads, text_heads = self_span // HEAD_DIM, text_span // HEAD_DIM

    def peer(step):
        return lax.rem(me + step, count)

    def near(step):
        return half * ring + lax.rem(place + step, ring)

    def self_cols(device):
        return pl.ds(pl.multiple_of(device * self_span, self_span), self_span)

    def text_cols(device):
        return pl.ds(pl.multiple_of(lax.rem(device, ring) * text_span, text_span), text_span)

    def remote(kind, step, source, target, device):
        return pltpu.make_async_remote_copy(
            src_ref=source,
            dst_ref=target,
            send_sem=send_sem.at[kind, step],
            recv_sem=recv_sem.at[kind, step],
            device_id={"seq": device},
            device_id_type=MESH,
        )

    kept = [
        pltpu.make_async_copy(text_q.at[0, :, text_cols(me)], text_rows.at[me], local_sem.at[0]),
        pltpu.make_async_copy(text_kv.at[0, :, :, text_cols(me)], context.at[place], local_sem.at[1]),
        pltpu.make_async_copy(self_q.at[0, :, self_cols(me)], own_q.at[me], local_sem.at[2]),
        pltpu.make_async_copy(self_k.at[0, :, self_cols(me)], own_k.at[me], local_sem.at[3]),
        pltpu.make_async_copy(self_v.at[0, :, self_cols(me)], own_v.at[me], local_sem.at[4]),
    ]
    for copy in kept:
        copy.start()

    barrier = pltpu.get_barrier_semaphore()
    for step in range(1, count):
        pl.semaphore_signal(barrier, inc=1, device_id={"seq": peer(step)}, device_id_type=MESH)
    pl.semaphore_wait(barrier, count - 1)

    text_in, self_in = [], []
    for step in range(1, count):
        to = peer(step)
        text_in.append(remote(0, step, text_q.at[0, :, text_cols(to)], text_rows.at[me], to))
    for step in range(1, ring):
        to = near(step)
        text_in.append(remote(1, step, text_kv.at[0, :, :, text_cols(to)], context.at[place], to))
    for kind, source, target in ((2, self_q, own_q), (3, self_k, own_k), (4, self_v, own_v)):
        for step in range(1, count):
            to = peer(step)
            self_in.append(remote(kind, step, source.at[0, :, self_cols(to)], target.at[me], to))
    order = [kind * (count - 1) + step - 1 for step in range(1, count) for kind in range(3)]
    for copy in text_in + [self_in[n] for n in order]:
        copy.start()

    for copy in kept[:2]:
        copy.wait()
    for copy in text_in:
        copy.wait_recv()
    length = text_len[branch]
    live = half * key_total + lax.broadcasted_iota(jnp.int32, (1, key_total), 1) < length
    lane = lax.broadcasted_iota(jnp.int32, (query_total, HEAD_DIM), 1)
    stats = jnp.full((query_total, HEAD_DIM), FAR, jnp.float32)
    for head in range(text_heads):
        span = slice(head * HEAD_DIM, (head + 1) * HEAD_DIM)
        mixed, top, total = attend(
            text_rows[:, :, span].reshape(query_total, HEAD_DIM),
            context[:, 0, :, span].reshape(key_total, HEAD_DIM),
            context[:, 1, :, span].reshape(key_total, HEAD_DIM),
            live,
        )
        safe = jnp.where(total > 0.0, total, 1.0)
        weight = jnp.where(total > 0.0, top + jnp.log(safe), FAR)
        text_part[:, :, span] = (mixed / safe).astype(jnp.bfloat16).reshape(count, rows, HEAD_DIM)
        stats = jnp.where(lane == head, weight, stats)
    stat_part[...] = stats.T[:text_heads]
    kept.append(pltpu.make_async_copy(text_part.at[me], text_back.at[half, :, text_cols(me)], local_sem.at[5]))
    kept.append(pltpu.make_async_copy(stat_part, stat_back.at[me], local_sem.at[6]))
    kept[5].start()
    kept[6].start()
    text_return = []
    for step in range(1, count):
        to = peer(step)
        text_return.append(remote(6, step, stat_part, stat_back.at[me], to))
        text_return.append(remote(5, step, text_part.at[to], text_back.at[half, :, text_cols(me)], to))
    for copy in text_return:
        copy.start()

    for copy in kept[2:5]:
        copy.wait()
    for copy in self_in:
        copy.wait_recv()
    for head in range(self_heads):
        span = slice(head * HEAD_DIM, (head + 1) * HEAD_DIM)
        mixed, top, total = attend(
            own_q[:, :, span].reshape(query_total, HEAD_DIM),
            own_k[:, :, span].reshape(query_total, HEAD_DIM),
            own_v[:, :, span].reshape(query_total, HEAD_DIM),
            None,
        )
        self_part[:, :, span] = (mixed / total).astype(jnp.bfloat16).reshape(count, rows, HEAD_DIM)
    kept.append(pltpu.make_async_copy(self_part.at[me], self_out.at[0, :, self_cols(me)], local_sem.at[7]))
    kept[7].start()
    self_return = []
    for step in range(1, count):
        to = peer(step)
        self_return.append(remote(7, step, self_part.at[to], self_out.at[0, :, self_cols(me)], to))
    for copy in self_return:
        copy.start()

    kept[5].wait()
    kept[6].wait()
    for copy in text_return:
        copy.wait_recv()
    stat_cols[...] = stat_back[...].reshape(HALVES * HEADS, query_total).T
    mine = stat_cols[pl.ds(pl.multiple_of(me * rows, rows), rows), :]
    sides = [mine[:, side * HEADS : (side + 1) * HEADS] for side in range(HALVES)]
    highest = functools.reduce(jnp.maximum, sides)
    shares = [jnp.exp(side - highest) for side in sides]
    whole = sum(shares)
    shares = [share / whole for share in shares]
    for head in range(HEADS):
        span = slice(head * HEAD_DIM, (head + 1) * HEAD_DIM)
        merged = sum(
            text_back[side, :, span].astype(jnp.float32) * shares[side][:, head : head + 1]
            for side in range(HALVES)
        )
        text_out[0, :, span] = merged.astype(jnp.bfloat16)

    kept[7].wait()
    for copy in self_return:
        copy.wait_recv()
    for copy in text_in + self_in + text_return + self_return:
        copy.wait_send()


def carry(*refs):
    sources, targets, held, sem = refs[0:2], refs[2:4], refs[4:6], refs[6]
    steps = []
    for n in range(2):
        steps.append(pltpu.make_async_copy(sources[n], held[n], sem.at[0, n]))
        steps[n].start()
    ends = []
    for n in range(2):
        steps[n].wait()
        ends.append(pltpu.make_async_copy(held[n], targets[n], sem.at[1, n]))
        ends[n].start()
    for end in ends:
        end.wait()


def fused_shards(self_queries, self_keys, self_values, text_queries, text_kv, text_len):
    count = lax.axis_size("seq")
    rows, channels = self_queries.shape[1:]
    context_rows = text_kv.shape[2]
    ring = count // HALVES
    self_span, text_span = channels // count, channels // ring
    in_place = pl.BlockSpec(memory_space=pl.ANY)
    bf16, f32 = jnp.bfloat16, jnp.float32
    out = jax.ShapeDtypeStruct((1, rows, channels), bf16)
    results = pl.pallas_call(
        functools.partial(fused, count),
        out_shape=(out, out),
        in_specs=[in_place] * 5 + [pl.BlockSpec(memory_space=pltpu.SMEM)],
        out_specs=(in_place, pl.BlockSpec(memory_space=pltpu.VMEM)),
        scratch_shapes=[
            pltpu.VMEM((count, rows, self_span), bf16),
            pltpu.VMEM((count, rows, self_span), bf16),
            pltpu.VMEM((count, rows, self_span), bf16),
            pltpu.VMEM((count, rows, text_span), bf16),
            pltpu.VMEM((ring, 2, context_rows, text_span), bf16),
            pltpu.VMEM((count, rows, self_span), bf16),
            pltpu.VMEM((count, rows, text_span), bf16),
            pltpu.VMEM((text_span // HEAD_DIM, count * rows), f32),
            pltpu.VMEM((HALVES, rows, channels), bf16),
            pltpu.VMEM((count, text_span // HEAD_DIM, count * rows), f32),
            pltpu.VMEM((count * rows, HALVES * HEADS), f32),
            pltpu.SemaphoreType.DMA((8, count)),
            pltpu.SemaphoreType.DMA((8, count)),
            pltpu.SemaphoreType.DMA((8,)),
        ],
        compiler_params=pltpu.CompilerParams(collective_id=0, has_side_effects=True),
        name="attention",
    )(self_queries, self_keys, self_values, text_queries, text_kv, text_len)
    return pl.pallas_call(
        carry,
        out_shape=(out, out),
        in_specs=[in_place] * 2,
        out_specs=(in_place, in_place),
        scratch_shapes=[
            pltpu.VMEM((1, rows, channels), bf16),
            pltpu.VMEM((1, rows, channels), bf16),
            pltpu.SemaphoreType.DMA((2, 2)),
        ],
        name="carry",
    )(*results)


def solution(mesh):
    count = mesh.shape["seq"]
    fits = count % HALVES == 0 and HEADS % count == 0
    return jax.shard_map(
        fused_shards if fits else shards,
        mesh=mesh,
        in_specs=(
            P("enc", ("groups", "seq"), None),
            P("enc", ("groups", "seq"), None),
            P("enc", ("groups", "seq"), None),
            P("enc", ("groups", "seq"), None),
            P("enc", None, ("groups", "seq"), None),
            P("groups"),
        ),
        out_specs=(P("enc", ("groups", "seq"), None), P("enc", ("groups", "seq"), None)),
        check_vma=False,
    )
```
